512 devices in a mesh: cuts: 8 (over y), row: 64 (over x, z, core).
Axes of the slice: x: 4, y: 8, z: 8, core: 2. Of those that a mesh axis runs over, the one named last changes fastest.
Arguments:
- block_tiles: float32 [192, 24, 128, 128], P('row'), may hold values from -0.109375 to 0.109375
- tile_pattern: int32 [192, 24], P('row'), may hold values from 0 to 191, as said below
- start_vectors: float32 [8, 32, 24576], P('cuts', None, 'row'), may hold values from -8 to 8
- centers: float32 [8], P('cuts'), may hold values from -0.3 to 0.3
- halfwidths: float32 [8], P('cuts'), may hold values from 0.9 to 1.3
- dup_pairs: int32 [8, 8, 2], P('cuts'), may hold values from 0 to 31, as said below
Outputs:
- filtered_basis: float32 [8, 32, 24576], P('cuts', None, 'row')
- projected: float32 [8, 32, 32], P('cuts')
The draws below stay inside these ranges and needn't reach their ends.
Inputs may be any that keep to these rules, and one draw needn't show every extreme that they name: tile_pattern[r, 0] = r; the other entries of block row r are distinct block rows, each within 12 of r cyclically and different from r. `dup_pairs`: within one slice the first entries of the pairs are distinct, and so are the second entries; the pairs of slice 0 are not used.
All inputs are finite; a program needn't handle non-finite values.
Results may differ from the reference program's by a relative error of at most 0.00015.
Values sent between devices are 32-bit elements; how exact they have to be, the bound alone decides.
A program may use at most 64 MiB of HBM per device.

```python
import math
import jax
import jax.numpy as jnp
from jax import lax

B = 128
K = 24
V = 32
DEG = 8
REACH = 12
PAIRS = 8
SLICES = 8
NB = 192
ORDER = 24576


def pair_table(key):

    def draw_slice(slice_key):
        own_index = jax.random.permutation(jax.random.fold_in(slice_key, 1), V)[:PAIRS]
        their_index = jax.random.permutation(jax.random.fold_in(slice_key, 2), V)[:PAIRS]
        return jnp.stack([own_index, their_index], axis=1)
    slice_keys = jax.random.split(jax.random.fold_in(key, 7), SLICES)
    return jax.vmap(draw_slice)(slice_keys).astype(jnp.int32)


def draw_dup_pairs(key, part):
    return pair_table(key)


def draw_tile_pattern(key, part):

    def draw_row(row_key, row_index):
        chosen = jax.random.permutation(row_key, 2 * REACH)[:K - 1].astype(jnp.int32)
        offsets = jnp.where(chosen < REACH, chosen - REACH, chosen - REACH + 1)
        return jnp.concatenate([row_index[None], (row_index + offsets) % NB])
    row_keys = jax.random.split(jax.random.fold_in(key, 3), NB)
    row_ids = jnp.arange(NB, dtype=jnp.int32)
    return jax.vmap(draw_row)(row_keys, row_ids).astype(jnp.int32)


def draw_start_vectors(key, part):
    full_shape = (SLICES, V, ORDER)
    base_draw = jnp.clip(jax.random.normal(jax.random.fold_in(key, 11), full_shape, jnp.float32), -6.0, 6.0)
    pairs = pair_table(key)
    own_index = pairs[:, :, 0]
    their_index = pairs[:, :, 1]
    previous = jnp.roll(base_draw, 1, axis=0)
    echoed = jnp.take_along_axis(previous, their_index[:, :, None], axis=1)
    own_rows = jnp.take_along_axis(base_draw, own_index[:, :, None], axis=1)
    blended = 0.8 * echoed + 0.6 * own_rows
    slice_ids = jnp.arange(SLICES, dtype=jnp.int32)[:, None]
    target = jnp.where(slice_ids[:, :, None] > 0, blended, own_rows)
    return base_draw.at[slice_ids, own_index].set(target)


def steps_of(own_key, dims, pieces, smallest, largest):
    def one(dim, parts):
        draws = jax.random.uniform(jax.random.fold_in(jax.random.fold_in(own_key, 6), dim), (parts,), jnp.float32, smallest / len(pieces), largest / len(pieces))
        return jnp.repeat(jnp.exp(draws), dims[dim] // parts).reshape((-1,) + (1,) * (len(dims) - dim - 1))

    level = one(*pieces[0])
    for cut in pieces[1:]:
        level = level * one(*cut)
    return level


def noise(rng, shape, deviation, most, pieces=(), kind=jnp.bfloat16):
    drawn = deviation * jax.random.normal(rng, shape, jnp.float32)
    if pieces:
        drawn = drawn * steps_of(rng, shape, pieces, -0.22, 0.18)
    return jnp.clip(drawn, -most, most).astype(kind)


def setup_inputs(seed: int = 0) -> dict:
    keys = jax.random.split(jax.random.key(seed), 7)
    block_tiles = noise(keys[0], (NB, K, B, B), (K * B) ** -0.5, 0.109375, ((0, 64),), jnp.float32)
    tile_pattern = draw_tile_pattern(jax.random.fold_in(keys[6], 71), 0)
    start_vectors = draw_start_vectors(jax.random.fold_in(keys[6], 71), 0)
    centers = jnp.clip(jax.random.uniform(keys[3], (SLICES,), jnp.float32, -0.3, 0.3) * steps_of(keys[3], (SLICES,), ((0, 8),), -0.4, 0.0), -0.3, 0.3)
    halfwidths = jnp.clip(0.9 + 0.39999998 * jax.random.uniform(keys[4], (SLICES,), jnp.float32) ** steps_of(keys[4], (SLICES,), ((0, 8),), -0.2, 0.2), 0.9, 1.3)
    dup_pairs = draw_dup_pairs(jax.random.fold_in(keys[6], 71), 0)
    return {"block_tiles": block_tiles, "tile_pattern": tile_pattern, "start_vectors": start_vectors, "centers": centers, "halfwidths": halfwidths, "dup_pairs": dup_pairs}


def apply_all(vectors, block_tiles, tile_pattern):
    vec_count = vectors.shape[0]
    blocks = vectors.reshape(vec_count, NB, B)
    picked = jnp.take(blocks, tile_pattern, axis=1)
    product = jnp.einsum('vrkc,rkdc->vrd', picked, block_tiles, precision=lax.Precision.HIGHEST)
    return product.reshape(vec_count, NB * B)

def lower_solve(factor, right_side):
    return lax.linalg.triangular_solve(factor, right_side, left_side=True, lower=True)

def one_slice(block_tiles, tile_pattern, slice_item):
    initial, center, halfwidth = slice_item
    previous = initial
    current = (apply_all(initial, block_tiles, tile_pattern) - center * initial) / halfwidth
    for degree in range(DEG - 1):
        following = 2.0 * (apply_all(current, block_tiles, tile_pattern) - center * current) / halfwidth - previous
        previous, current = (current, following)
    gram_matrix = jnp.dot(current, current.T, precision=lax.Precision.HIGHEST)
    factor = jnp.linalg.cholesky(gram_matrix)
    basis_raw = math.sqrt(ORDER) * lower_solve(factor, current)
    imaged = apply_all(basis_raw, block_tiles, tile_pattern)
    projected = jnp.dot(basis_raw, imaged.T, precision=lax.Precision.HIGHEST) / ORDER
    return (basis_raw, projected)

def reference(block_tiles, tile_pattern, start_vectors, centers, halfwidths, dup_pairs):
    basis_raw, projected = lax.map(lambda slice_item: one_slice(block_tiles, tile_pattern, slice_item), (start_vectors, centers, halfwidths))
    columns = jnp.arange(V, dtype=jnp.int32)
    own_index = dup_pairs[:, :, 0]
    their_index = dup_pairs[:, :, 1]
    selector = (their_index[:, :, None] == columns[None, None, :]).astype(jnp.float32)
    target_mask = (own_index[:, :, None] == columns[None, None, :]).astype(jnp.float32)
    lower_basis = jnp.concatenate([jnp.zeros((1, V, ORDER), jnp.float32), basis_raw[:-1]], axis=0)
    lower_rows = jnp.einsum('spv,svn->spn', selector, lower_basis, precision=lax.Precision.HIGHEST)
    correlation = jnp.einsum('spn,svn->spv', lower_rows, basis_raw, precision=lax.Precision.HIGHEST) / ORDER
    filtered_basis = basis_raw - jnp.einsum('spv,spn->svn', target_mask * correlation, lower_rows, precision=lax.Precision.HIGHEST)
    return (filtered_basis, projected)
```

```python
import functools
import math

import jax
import jax.numpy as jnp
from jax import lax
from jax.experimental import pallas as pl
from jax.experimental.pallas import tpu as pltpu
from jax.sharding import PartitionSpec as P

DEG = 8
REACH = 12
B = 128
K = 24
R = 3
SPAN = R * 9
V = 32
GROUPS = 2
GV = V // GROUPS
W = R * B
MESH = pl.DeviceIdType.MESH
HIGH = lax.Precision.HIGHEST
F32 = jnp.float32
BF16 = jnp.bfloat16

ORDER = (0, 1, 2, -2, -1, 3, 4, -4, -3)
SLOT = {m: i for i, m in enumerate(ORDER)}
DIRECT = ((2, -2), (-2, 2), (4, -4), (-4, 4), (-3, -3), (1, 1))
FORWARD = ((2, -1), (-2, 3))
NSEND = len(DIRECT) + len(FORWARD)


def split(values):
    high = values.astype(BF16)
    low = (values - high.astype(F32)).astype(BF16)
    return high, low


def stacked(pieces):
    columns = []
    for piece in pieces:
        columns.append(jnp.concatenate(split(piece), axis=0))
    return jnp.concatenate(columns, axis=1)


def nt(a, b):
    return lax.dot_general(
        a, b, (((1,), (1,)), ((), ())), precision=HIGH, preferred_element_type=F32
    )


def nn(a, b):
    return jnp.dot(a, b, precision=HIGH, preferred_element_type=F32)


def kernel(
    order_total,
    tiles_hbm,
    pattern,
    start_hbm,
    center_ref,
    half_ref,
    pairs,
    out_ref,
    proj_ref,
    tiles,
    weights,
    inverse,
    held,
    halo,
    low,
    zbuf,
    xbuf,
    cbuf,
    tile_sem,
    start_sem,
    send_sem,
    recv_sem,
    low_send,
    low_recv,
    z_send,
    z_recv,
    x_send,
    x_recv,
    c_send,
    c_recv,
):
    me = lax.axis_index("row")
    cut = lax.axis_index("cuts")
    core = lax.rem(me, 2)
    chip = me // 2
    zpos = lax.rem(chip, 8)
    xpos = chip // 8
    sign = 1 - 2 * core

    def at(m):
        return {"row": lax.rem(me + m * sign + 64, 64)}

    def cut_at(step):
        return {"cuts": lax.rem(cut + step + 8, 8)}

    loads = []
    for g in range(GROUPS):
        load = pltpu.make_async_copy(
            start_hbm.at[0, pl.ds(g * GV, GV), :], held.at[g, 0], start_sem.at[g]
        )
        load.start()
        loads.append(load)
    tile_loads = []
    for i in range(R):
        load = pltpu.make_async_copy(tiles_hbm.at[i], tiles.at[i], tile_sem.at[i])
        load.start()
        tile_loads.append(load)

    barrier = pltpu.get_barrier_semaphore()
    for m in (-4, -3, -2, -1, 1, 2, 3, 4):
        pl.semaphore_signal(barrier, inc=1, device_id=at(m), device_id_type=MESH)
    for step in (-1, 1):
        pl.semaphore_signal(barrier, inc=1, device_id=cut_at(step), device_id_type=MESH)
    pl.semaphore_wait(barrier, 10)

    def remote(src, g, p, coordinate, target, index):
        return pltpu.make_async_remote_copy(
            src_ref=src,
            dst_ref=halo.at[g, p, SLOT[coordinate]],
            send_sem=send_sem.at[g, index],
            recv_sem=recv_sem.at[g, p, SLOT[coordinate]],
            device_id=at(target),
            device_id_type=MESH,
        )

    def direct(g, p, index):
        target, coordinate = DIRECT[index]
        return remote(held.at[g, p], g, p, coordinate, target, index)

    def forward(g, p, index):
        source, coordinate = FORWARD[index]
        return remote(
            halo.at[g, p, SLOT[source]], g, p, coordinate, 1, len(DIRECT) + index
        )

    def arrived(g, p, m):
        remote(held.at[g, p], g, p, m, 1, 0).wait_recv()

    def send(g, p):
        for index in range(len(DIRECT)):
            direct(g, p, index).start()

    for g in range(GROUPS):
        loads[g].wait()
        send(g, 0)
    for g in range(GROUPS):
        held[g, 1] = jnp.zeros((GV, W), F32)

    lowest = R * me - REACH

    def find(n, carry):
        i = n // SPAN
        t = n - i * SPAN
        column = lax.rem(lowest + t + 192, 192)
        found = jnp.int32(-1)
        for k in range(K):
            found = jnp.where(pattern[i, k] == column, k, found)
        inverse[n] = found
        return carry

    lax.fori_loop(0, R * SPAN, find, 0)

    for load in tile_loads:
        load.wait()

    for j, m in enumerate(ORDER):

        def build(b, carry, j=j, m=m):
            for i in range(R):
                t = R * m * sign + REACH + b
                index = inverse[i * SPAN + t]
                tile = tiles[i, jnp.maximum(index, 0)]
                tile = jnp.where(index >= 0, tile, 0.0)
                high, rest = split(tile.T)
                rows = pl.ds(pl.multiple_of(j * W + b * B, B), B)
                weights[rows, pl.ds(i * 2 * B, B)] = high
                weights[rows, pl.ds(i * 2 * B + B, B)] = rest
            return carry

        lax.fori_loop(0, R, build, 0)

    def product(g, p):
        def chunk(first, count):
            pieces = []
            for j in range(first, first + count):
                pieces.append(held[g, p] if j == 0 else halo[g, p, j])
            return jnp.dot(
                stacked(pieces),
                weights[pl.ds(first * W, count * W), :],
                preferred_element_type=F32,
            )

        for index, (source, _) in enumerate(FORWARD):
            arrived(g, p, source)
            forward(g, p, index).start()
        arrived(g, p, 1)
        total = chunk(0, 4)
        arrived(g, p, -1)
        arrived(g, p, 3)
        total += chunk(4, 2)
        arrived(g, p, 4)
        arrived(g, p, -4)
        arrived(g, p, -3)
        total += chunk(6, 3)
        columns = []
        for i in range(R):
            both = total[:, i * 2 * B : i * 2 * B + B] + total[:, i * 2 * B + B : (i + 1) * 2 * B]
            columns.append(both[:GV] + both[GV:])
        return jnp.concatenate(columns, axis=1)

    def sent(g, p):
        for index in range(len(DIRECT)):
            direct(g, p, index).wait_send()
        for index in range(len(FORWARD)):
            forward(g, p, index).wait_send()

    center = center_ref[0]
    inverse_half = 1.0 / jnp.full((GV, W), half_ref[0], F32)

    def steps(n, carry):
        for p in (0, 1):
            factor = jnp.where(n * 2 + p == 0, 1.0, 2.0).astype(F32)
            for g in range(GROUPS):
                applied = product(g, p)
                following = (
                    factor * (applied - center * held[g, p]) * inverse_half - held[g, 1 - p]
                )
                sent(g, p)
                held[g, 1 - p] = following
                send(g, 1 - p)
        return carry

    lax.fori_loop(0, DEG // 2, steps, 0)

    def to_next(g):
        return pltpu.make_async_remote_copy(
            src_ref=held.at[g, 0],
            dst_ref=low.at[g],
            send_sem=low_send.at[g],
            recv_sem=low_recv.at[g],
            device_id=cut_at(1),
            device_id_type=MESH,
        )

    for g in range(GROUPS):
        to_next(g).start()
    imaged = []
    for g in range(GROUPS):
        imaged.append(product(g, 0))
        sent(g, 0)
    imaged = jnp.concatenate(imaged, axis=0)
    for g in range(GROUPS):
        to_next(g).wait()
    current = jnp.concatenate([held[g, 0] for g in range(GROUPS)], axis=0)
    lower = jnp.concatenate([low[g] for g in range(GROUPS)], axis=0)
    none = jnp.zeros((V, W), F32)
    partial = nt(current, jnp.concatenate([current, lower, imaged, none], axis=0)) + nt(
        lower, jnp.concatenate([none, none, none, lower], axis=0)
    )

    def gather(value, buffer, count, own, send_sems, recv_sems, device):
        buffer[own] = value
        copies = []
        for step in range(1, count):
            there = lax.rem(own + step, count)
            copy = pltpu.make_async_remote_copy(
                src_ref=buffer.at[own],
                dst_ref=buffer.at[own],
                send_sem=send_sems.at[step],
                recv_sem=recv_sems.at[step],
                device_id={"row": device(there)},
                device_id_type=MESH,
            )
            copy.start()
            copies.append(copy)
        for copy in copies:
            copy.wait()
        total = buffer[0]
        for n in range(1, count):
            total = total + buffer[n]
        return total

    total = gather(partial, zbuf, 8, zpos, z_send, z_recv, lambda z: (xpos * 8 + z) * 2 + core)
    total = gather(total, xbuf, 4, xpos, x_send, x_recv, lambda x: (x * 8 + zpos) * 2 + core)
    total = gather(total, cbuf, 2, core, c_send, c_recv, lambda k: chip * 2 + k)

    lane = lax.broadcasted_iota(jnp.int32, (V, 4 * V), 1)
    row = lax.broadcasted_iota(jnp.int32, (V, 4 * V), 0)
    unit = jnp.where((lane == row + V) | (lane == row + 2 * V), 1.0, 0.0).astype(F32)
    inner = (lane >= V) & (lane < 3 * V)
    left = lane < 2 * V
    table = jnp.where(inner, unit, total)
    for j in range(V - 1):
        pivot_row = table[j : j + 1, :]
        column = jnp.where(left, table[:, j : j + 1], table[:, 3 * V + j : 3 * V + j + 1])
        pivot = jnp.where(
            left[:1], pivot_row[:, j : j + 1], pivot_row[:, 3 * V + j : 3 * V + j + 1]
        )
        scaled = pivot_row / pivot
        table = table - jnp.where(row > j, column * scaled, 0.0)
    diagonal_left = jnp.sum(jnp.where(lane == row, table, 0.0), axis=1, keepdims=True)
    diagonal_right = jnp.sum(jnp.where(lane == row + 3 * V, table, 0.0), axis=1, keepdims=True)
    table = table / jnp.sqrt(jnp.where(left, diagonal_left, diagonal_right))
    table = jnp.where(inner, table, 0.0)
    factor_inverse = pltpu.roll(table, 3 * V, 1)[:, :V]
    lower_inverse = pltpu.roll(table, 2 * V, 1)[:, :V]
    half_way = nn(factor_inverse, total)
    cross = nt(pltpu.roll(half_way, 3 * V, 1)[:, :V], lower_inverse)
    proj_ref[0] = nt(pltpu.roll(half_way, 2 * V, 1)[:, :V], factor_inverse)
    small_row = lax.broadcasted_iota(jnp.int32, (V, V), 0)
    small_lane = lax.broadcasted_iota(jnp.int32, (V, V), 1)
    chosen = jnp.zeros((V, V), F32)
    for p in range(8):
        chosen += jnp.where(
            (small_row == pairs[0, p, 0]) & (small_lane == pairs[0, p, 1]), 1.0, 0.0
        )
    removed = nn(chosen * cross, table)
    removed = jnp.where(cut > 0, removed, 0.0)
    mixing = jnp.where(left, table, -removed)
    lower = jnp.where(cut > 0, lower, 0.0)
    out_ref[0] = math.sqrt(order_total) * nn(
        mixing, jnp.concatenate([none, current, lower, none], axis=0)
    )


def local(block_tiles, tile_pattern, start_vectors, centers, halfwidths, dup_pairs):
    order_total = start_vectors.shape[2] * lax.axis_size("row")
    smem = pl.BlockSpec(memory_space=pltpu.SMEM)
    vmem = pl.BlockSpec(memory_space=pltpu.VMEM)
    anywhere = pl.BlockSpec(memory_space=pl.ANY)
    dma = pltpu.SemaphoreType.DMA
    return pl.pallas_call(
        functools.partial(kernel, order_total),
        out_shape=(
            jax.ShapeDtypeStruct((1, V, W), F32),
            jax.ShapeDtypeStruct((1, V, V), F32),
        ),
        in_specs=[anywhere, smem, anywhere, smem, smem, smem],
        out_specs=(vmem, vmem),
        scratch_shapes=[
            pltpu.VMEM((R, K, B, B), F32),
            pltpu.VMEM((9 * W, 2 * W), BF16),
            pltpu.SMEM((R * SPAN,), jnp.int32),
            pltpu.VMEM((GROUPS, 2, GV, W), F32),
            pltpu.VMEM((GROUPS, 2, 9, GV, W), F32),
            pltpu.VMEM((GROUPS, GV, W), F32),
            pltpu.VMEM((8, V, 4 * V), F32),
            pltpu.VMEM((4, V, 4 * V), F32),
            pltpu.VMEM((2, V, 4 * V), F32),
            dma((R,)),
            dma((GROUPS,)),
            dma((GROUPS, NSEND)),
            dma((GROUPS, 2, 9)),
            dma((GROUPS,)),
            dma((GROUPS,)),
            dma((8,)),
            dma((8,)),
            dma((4,)),
            dma((4,)),
            dma((2,)),
            dma((2,)),
        ],
        compiler_params=pltpu.CompilerParams(
            collective_id=0, has_side_effects=True, vmem_limit_bytes=48 << 20
        ),
    )(block_tiles, tile_pattern, start_vectors, centers, halfwidths, dup_pairs)


def solution(mesh):
    in_specs = (
        P("row", None, None, None),
        P("row", None),
        P("cuts", None, "row"),
        P("cuts"),
        P("cuts"),
        P("cuts", None, None),
    )
    out_specs = (P("cuts", None, "row"), P("cuts", None, None))
    return jax.shard_map(local, mesh=mesh, in_specs=in_specs, out_specs=out_specs, check_vma=False)
```

```python
import functools
import math

import jax
import jax.numpy as jnp
from jax import lax
from jax.experimental import pallas as pl
from jax.experimental.pallas import tpu as pltpu
from jax.sharding import PartitionSpec as P

DEG = 8
REACH = 12
B = 128
K = 24
R = 3
SPAN = R * 9
V = 32
GROUPS = 2
GV = V // GROUPS
W = R * B
MESH = pl.DeviceIdType.MESH
HIGH = lax.Precision.HIGHEST
F32 = jnp.float32
BF16 = jnp.bfloat16

ORDER = (0, 1, 2, -2, -1, 3, 4, -4, -3)
SLOT = {m: i for i, m in enumerate(ORDER)}
DIRECT = ((2, -2), (-2, 2), (4, -4), (-4, 4), (-3, -3), (1, 1))
FORWARD = ((2, -1), (-2, 3))
NSEND = len(DIRECT) + len(FORWARD)


def split(values):
    high = values.astype(BF16)
    low = (values - high.astype(F32)).astype(BF16)
    return high, low


def stacked(pieces):
    columns = []
    for piece in pieces:
        columns.append(jnp.concatenate(split(piece), axis=0))
    return jnp.concatenate(columns, axis=1)


def nt(a, b):
    return lax.dot_general(
        a, b, (((1,), (1,)), ((), ())), precision=HIGH, preferred_element_type=F32
    )


def nn(a, b):
    return jnp.dot(a, b, precision=HIGH, preferred_element_type=F32)


def kernel(
    order_total,
    tiles_hbm,
    pattern_hbm,
    start_hbm,
    center_hbm,
    half_hbm,
    pairs_hbm,
    out_ref,
    proj_ref,
    pattern,
    center_ref,
    half_ref,
    pairs,
    tiles,
    weights,
    inverse,
    held,
    halo,
    low,
    zbuf,
    xbuf,
    cbuf,
    tile_sem,
    start_sem,
    send_sem,
    recv_sem,
    low_send,
    low_recv,
    z_send,
    z_recv,
    x_send,
    x_recv,
    c_send,
    c_recv,
    factor_buf,
    factor_sem,
    small_sem,
):
    me = lax.axis_index("row")
    cut = lax.axis_index("cuts")
    core = lax.rem(me, 2)
    chip = me // 2
    zpos = lax.rem(chip, 8)
    xpos = chip // 8
    sign = 1 - 2 * core

    def at(m):
        return {"row": lax.rem(me + m * sign + 64, 64)}

    def cut_at(step):
        return {"cuts": lax.rem(cut + step + 8, 8)}

    small_loads = []
    for n, (source, target) in enumerate(
        (
            (pattern_hbm, pattern),
            (center_hbm, center_ref),
            (half_hbm, half_ref),
            (pairs_hbm, pairs),
        )
    ):
        load = pltpu.make_async_copy(source, target, small_sem.at[n])
        load.start()
        small_loads.append(load)
    loads = []
    for g in range(GROUPS):
        load = pltpu.make_async_copy(
            start_hbm.at[0, pl.ds(g * GV, GV), :], held.at[g, 0], start_sem.at[g]
        )
        load.start()
        loads.append(load)
    tile_loads = []
    for i in range(R):
        load = pltpu.make_async_copy(tiles_hbm.at[i], tiles.at[i], tile_sem.at[i])
        load.start()
        tile_loads.append(load)

    barrier = pltpu.get_barrier_semaphore()
    for m in (-4, -3, -2, -1, 1, 2, 3, 4):
        pl.semaphore_signal(barrier, inc=1, device_id=at(m), device_id_type=MESH)
    for step in (-1, 1):
        pl.semaphore_signal(barrier, inc=1, device_id=cut_at(step), device_id_type=MESH)
    pl.semaphore_wait(barrier, 10)

    def remote(src, g, p, coordinate, target, index):
        return pltpu.make_async_remote_copy(
            src_ref=src,
            dst_ref=halo.at[g, p, SLOT[coordinate]],
            send_sem=send_sem.at[g, index],
            recv_sem=recv_sem.at[g, p, SLOT[coordinate]],
            device_id=at(target),
            device_id_type=MESH,
        )

    def direct(g, p, index):
        target, coordinate = DIRECT[index]
        return remote(held.at[g, p], g, p, coordinate, target, index)

    def forward(g, p, index):
        source, coordinate = FORWARD[index]
        return remote(
            halo.at[g, p, SLOT[source]], g, p, coordinate, 1, len(DIRECT) + index
        )

    def arrived(g, p, m):
        remote(held.at[g, p], g, p, m, 1, 0).wait_recv()

    def send(g, p):
        for index in range(len(DIRECT)):
            direct(g, p, index).start()

    for g in range(GROUPS):
        loads[g].wait()
        send(g, 0)
    for g in range(GROUPS):
        held[g, 1] = jnp.zeros((GV, W), F32)

    for load in small_loads:
        load.wait()

    lowest = R * me - REACH

    def find(n, carry):
        i = n // SPAN
        t = n - i * SPAN
        column = lax.rem(lowest + t + 192, 192)
        found = jnp.int32(-1)
        for k in range(K):
            found = jnp.where(pattern[i, k] == column, k, found)
        inverse[n] = found
        return carry

    lax.fori_loop(0, R * SPAN, find, 0)

    for load in tile_loads:
        load.wait()

    def build(j, carry):
        m = jnp.int32(0)
        for slot, source in enumerate(ORDER):
            m = jnp.where(j == slot, source, m)
        for b in range(R):
            rows = pl.ds(pl.multiple_of(j * W + b * B, B), B)
            for i in range(R):
                index = inverse[i * SPAN + R * m * sign + REACH + b]
                tile = tiles[i, jnp.maximum(index, 0)]
                tile = jnp.where(index >= 0, tile, 0.0)
                high, rest = split(tile.T)
                weights[rows, pl.ds(i * 2 * B, B)] = high
                weights[rows, pl.ds(i * 2 * B + B, B)] = rest
        return carry

    lax.fori_loop(0, len(ORDER), build, 0)

    def product(g, p):
        def chunk(first, count):
            pieces = []
            for j in range(first, first + count):
                pieces.append(held[g, p] if j == 0 else halo[g, p, j])
            return jnp.dot(
                stacked(pieces),
                weights[pl.ds(first * W, count * W), :],
                preferred_element_type=F32,
            )

        arrived(g, p, 1)
        total = chunk(0, 4)
        arrived(g, p, -1)
        arrived(g, p, 3)
        total += chunk(4, 2)
        arrived(g, p, 4)
        arrived(g, p, -4)
        arrived(g, p, -3)
        total += chunk(6, 3)
        columns = []
        for i in range(R):
            both = total[:, i * 2 * B : i * 2 * B + B] + total[:, i * 2 * B + B : (i + 1) * 2 * B]
            columns.append(both[:GV] + both[GV:])
        return jnp.concatenate(columns, axis=1)

    def pass_on(g, p):
        for index, (source, _) in enumerate(FORWARD):
            arrived(g, p, source)
            forward(g, p, index).start()

    def sent(g, p):
        for index in range(len(DIRECT)):
            direct(g, p, index).wait_send()
        for index in range(len(FORWARD)):
            forward(g, p, index).wait_send()

    center = center_ref[0]
    inverse_half = 1.0 / jnp.full((GV, W), half_ref[0], F32)

    def steps(n, carry):
        for p in (0, 1):
            factor = jnp.where(n * 2 + p == 0, 1.0, 2.0).astype(F32)
            for g in range(GROUPS):
                pass_on(g, p)
                applied = product(g, p)
                following = (
                    factor * (applied - center * held[g, p]) * inverse_half - held[g, 1 - p]
                )
                sent(g, p)
                held[g, 1 - p] = following
                send(g, 1 - p)
        return carry

    lax.fori_loop(0, DEG // 2, steps, 0)

    def to_next(g):
        return pltpu.make_async_remote_copy(
            src_ref=held.at[g, 0],
            dst_ref=low.at[g],
            send_sem=low_send.at[g],
            recv_sem=low_recv.at[g],
            device_id=cut_at(1),
            device_id_type=MESH,
        )

    for g in range(GROUPS):
        to_next(g).start()
    current = jnp.concatenate([held[g, 0] for g in range(GROUPS)], axis=0)

    def narrow(left, right):
        none = jnp.zeros((3 * V, W), F32)
        value = nt(left, jnp.concatenate([right, none], axis=0))
        return packed(value)

    def packed(value):
        total = value[:8]
        for q in range(1, 4):
            total = total + pltpu.roll(value[8 * q : 8 * q + 8], V * q, 1)
        return total

    def unpacked(value):
        parts = [value] + [pltpu.roll(value, 4 * V - V * q, 1) for q in range(1, 4)]
        return jnp.concatenate(parts, axis=0)

    def copies(a, phase):
        buffer, send_sems, recv_sems, own, device = phase
        count = buffer.shape[1]
        result = []
        for step in range(1, count):
            there = lax.rem(own + step, count)
            result.append(
                pltpu.make_async_remote_copy(
                    src_ref=buffer.at[a, own],
                    dst_ref=buffer.at[a, own],
                    send_sem=send_sems.at[a, step],
                    recv_sem=recv_sems.at[a, step],
                    device_id={"row": device(there)},
                    device_id_type=MESH,
                )
            )
        return result

    def begin(a, phase, value):
        phase[0][a, phase[3]] = value
        for copy in copies(a, phase):
            copy.start()

    def finish(a, phase):
        for copy in copies(a, phase):
            copy.wait()
        total = phase[0][a, 0]
        for n in range(1, phase[0].shape[1]):
            total = total + phase[0][a, n]
        return total

    along_z = (zbuf, z_send, z_recv, zpos, lambda z: (xpos * 8 + z) * 2 + core)
    along_x = (xbuf, x_send, x_recv, xpos, lambda x: (x * 8 + zpos) * 2 + core)
    in_chip = (cbuf, c_send, c_recv, core, lambda k: chip * 2 + k)

    GRAM, CROSS, QUOTIENT = 0, 1, 2
    begin(GRAM, along_z, narrow(current, current))
    pass_on(0, 0)
    imaged = [product(0, 0)]
    pass_on(1, 0)
    for g in range(GROUPS):
        to_next(g).wait()
    lower = jnp.concatenate([low[g] for g in range(GROUPS)], axis=0)
    begin(CROSS, along_z, narrow(current, lower))
    begin(GRAM, along_x, finish(GRAM, along_z))
    imaged.append(product(1, 0))
    begin(QUOTIENT, along_z, narrow(current, jnp.concatenate(imaged, axis=0)))
    for g in range(GROUPS):
        sent(g, 0)
    begin(CROSS, along_x, finish(CROSS, along_z))
    begin(GRAM, in_chip, finish(GRAM, along_x))
    gram = unpacked(finish(GRAM, in_chip))

    lane = lax.broadcasted_iota(jnp.int32, (V, 4 * V), 1)
    row = lax.broadcasted_iota(jnp.int32, (V, 4 * V), 0)
    table = jnp.where(lane < V, gram, jnp.where(lane == row + V, 1.0, 0.0))

    def eliminate(table, first, last):
        for j in range(first, last):
            scaled = table[j : j + 1, :] / table[j : j + 1, j : j + 1]
            table = table - jnp.where(row > j, table[:, j : j + 1] * scaled, 0.0)
        return table

    table = eliminate(table, 0, V // 2)
    begin(QUOTIENT, along_x, finish(QUOTIENT, along_z))
    table = eliminate(table, V // 2, V - 1)
    diagonal = jnp.sum(jnp.where(lane == row, table, 0.0), axis=1, keepdims=True)
    table = jnp.where(lane < V, 0.0, table) / jnp.sqrt(diagonal)
    table = pltpu.roll(table, 3 * V, 1)
    factor_buf[0] = packed(table)
    factor_copy = pltpu.make_async_remote_copy(
        src_ref=factor_buf.at[0],
        dst_ref=factor_buf.at[1],
        send_sem=factor_sem.at[0],
        recv_sem=factor_sem.at[1],
        device_id=cut_at(1),
        device_id_type=MESH,
    )
    factor_copy.start()
    factor_inverse = table[:, :V]
    begin(CROSS, in_chip, finish(CROSS, along_x))
    basis = nn(factor_inverse, current)
    small_row = lax.broadcasted_iota(jnp.int32, (V, V), 0)
    small_lane = lax.broadcasted_iota(jnp.int32, (V, V), 1)
    chosen = jnp.zeros((V, V), F32)
    for p in range(8):
        chosen += jnp.where(
            (small_row == pairs[0, 0, p]) & (small_lane == pairs[0, 1, p]), 1.0, 0.0
        )
    begin(QUOTIENT, in_chip, finish(QUOTIENT, along_x))
    cross = nn(factor_inverse, unpacked(finish(CROSS, in_chip))[:, :V])
    factor_copy.wait()
    lower_inverse = unpacked(factor_buf[1])[:, :V]
    lower_basis = jnp.where(cut > 0, nn(lower_inverse, lower), 0.0)
    removed = jnp.where(cut > 0, chosen * nt(cross, lower_inverse), 0.0)
    out_ref[0] = math.sqrt(order_total) * (basis - nn(removed, lower_basis))
    quotient = unpacked(finish(QUOTIENT, in_chip))[:, :V]
    proj_ref[0] = nt(nn(factor_inverse, quotient), factor_inverse)


def local(block_tiles, tile_pattern, start_vectors, centers, halfwidths, dup_pairs):
    order_total = start_vectors.shape[2] * lax.axis_size("row")
    vmem = pl.BlockSpec(memory_space=pltpu.VMEM)
    hbm = pl.BlockSpec(memory_space=pltpu.HBM)
    dma = pltpu.SemaphoreType.DMA
    return pl.pallas_call(
        functools.partial(kernel, order_total),
        out_shape=(
            jax.ShapeDtypeStruct((1, V, W), F32),
            jax.ShapeDtypeStruct((1, V, V), F32),
        ),
        in_specs=[hbm] * 6,
        out_specs=(vmem, vmem),
        scratch_shapes=[
            pltpu.SMEM((R, K), jnp.int32),
            pltpu.SMEM((1,), F32),
            pltpu.SMEM((1,), F32),
            pltpu.SMEM((1, 2, 8), jnp.int32),
            pltpu.VMEM((R, K, B, B), F32),
            pltpu.VMEM((9 * W, 2 * W), BF16),
            pltpu.SMEM((R * SPAN,), jnp.int32),
            pltpu.VMEM((GROUPS, 2, GV, W), F32),
            pltpu.VMEM((GROUPS, 2, 9, GV, W), F32),
            pltpu.VMEM((GROUPS, GV, W), F32),
            pltpu.VMEM((3, 8, 8, 4 * V), F32),
            pltpu.VMEM((3, 4, 8, 4 * V), F32),
            pltpu.VMEM((3, 2, 8, 4 * V), F32),
            dma((R,)),
            dma((GROUPS,)),
            dma((GROUPS, NSEND)),
            dma((GROUPS, 2, 9)),
            dma((GROUPS,)),
            dma((GROUPS,)),
            dma((3, 8)),
            dma((3, 8)),
            dma((3, 4)),
            dma((3, 4)),
            dma((3, 2)),
            dma((3, 2)),
            pltpu.VMEM((2, 8, 4 * V), F32),
            dma((2,)),
            dma((4,)),
        ],
        compiler_params=pltpu.CompilerParams(
            collective_id=0, has_side_effects=True, vmem_limit_bytes=60 << 20
        ),
    )(
        block_tiles,
        tile_pattern,
        start_vectors,
        centers,
        halfwidths,
        jnp.transpose(dup_pairs, (0, 2, 1)),
    )


def solution(mesh):
    in_specs = (
        P("row", None, None, None),
        P("row", None),
        P("cuts", None, "row"),
        P("cuts"),
        P("cuts"),
        P("cuts", None, None),
    )
    out_specs = (P("cuts", None, "row"), P("cuts", None, None))
    return jax.shard_map(local, mesh=mesh, in_specs=in_specs, out_specs=out_specs, check_vma=False)
```

```python
import functools
import math

import jax
import jax.numpy as jnp
from jax import lax
from jax.experimental import pallas as pl
from jax.experimental.pallas import tpu as pltpu
from jax.sharding import PartitionSpec as P

DEG = 8
REACH = 12
B = 128
K = 24
R = 3
SPAN = R * 9
V = 32
GROUPS = 2
GV = V // GROUPS
W = R * B
MESH = pl.DeviceIdType.MESH
HIGH = lax.Precision.HIGHEST
F32 = jnp.float32
BF16 = jnp.bfloat16

ORDER = (0, 1, 2, -2, -1, 3, -4, 4, -3)
SLOT = {m: i for i, m in enumerate(ORDER)}
DIRECT = ((2, -2), (-2, 2), (4, -4), (-4, 4), (-3, -3), (1, 1))
FORWARD = ((2, -1), (-2, 3))
NSEND = len(DIRECT) + len(FORWARD)


def split(values):
    high = values.astype(BF16)
    low = (values - high.astype(F32)).astype(BF16)
    return high, low


def stacked(pieces):
    columns = []
    for piece in pieces:
        columns.append(jnp.concatenate(split(piece), axis=0))
    return jnp.concatenate(columns, axis=1)


def nt(a, b):
    return lax.dot_general(
        a, b, (((1,), (1,)), ((), ())), precision=HIGH, preferred_element_type=F32
    )


def nn(a, b):
    return jnp.dot(a, b, precision=HIGH, preferred_element_type=F32)


def kernel(
    order_total,
    tiles_hbm,
    pattern_hbm,
    start_hbm,
    center_hbm,
    half_hbm,
    pairs_hbm,
    out_ref,
    proj_ref,
    pattern,
    center_ref,
    half_ref,
    pairs,
    tiles,
    weights,
    inverse,
    held,
    halo,
    low,
    zbuf,
    xbuf,
    cbuf,
    tile_sem,
    start_sem,
    send_sem,
    recv_sem,
    low_send,
    low_recv,
    z_send,
    z_recv,
    x_send,
    x_recv,
    c_send,
    c_recv,
    factor_buf,
    factor_sem,
    small_sem,
):
    me = lax.axis_index("row")
    cut = lax.axis_index("cuts")
    core = lax.rem(me, 2)
    chip = me // 2
    zpos = lax.rem(chip, 8)
    xpos = chip // 8
    sign = 1 - 2 * core

    def at(m):
        return {"row": lax.rem(me + m * sign + 64, 64)}

    def cut_at(step):
        return {"cuts": lax.rem(cut + step + 8, 8)}

    small_loads = []
    for n, (source, target) in enumerate(
        (
            (pattern_hbm, pattern),
            (center_hbm, center_ref),
            (half_hbm, half_ref),
            (pairs_hbm, pairs),
        )
    ):
        load = pltpu.make_async_copy(source, target, small_sem.at[n])
        load.start()
        small_loads.append(load)
    loads = []
    for g in range(GROUPS):
        load = pltpu.make_async_copy(
            start_hbm.at[0, pl.ds(g * GV, GV), :], held.at[g, 0], start_sem.at[g]
        )
        load.start()
        loads.append(load)
    tile_loads = []
    for i in range(R):
        load = pltpu.make_async_copy(tiles_hbm.at[i], tiles.at[i], tile_sem.at[i])
        load.start()
        tile_loads.append(load)

    barrier = pltpu.get_barrier_semaphore()
    for m in (-4, -3, -2, -1, 1, 2, 3, 4):
        pl.semaphore_signal(barrier, inc=1, device_id=at(m), device_id_type=MESH)
    for step in (-1, 1):
        pl.semaphore_signal(barrier, inc=1, device_id=cut_at(step), device_id_type=MESH)
    pl.semaphore_wait(barrier, 10)

    def remote(src, g, p, coordinate, target, index):
        return pltpu.make_async_remote_copy(
            src_ref=src,
            dst_ref=halo.at[g, p, SLOT[coordinate]],
            send_sem=send_sem.at[g, index],
            recv_sem=recv_sem.at[g, p, SLOT[coordinate]],
            device_id=at(target),
            device_id_type=MESH,
        )

    def direct(g, p, index):
        target, coordinate = DIRECT[index]
        return remote(held.at[g, p], g, p, coordinate, target, index)

    def forward(g, p, index):
        source, coordinate = FORWARD[index]
        return remote(
            halo.at[g, p, SLOT[source]], g, p, coordinate, 1, len(DIRECT) + index
        )

    def arrived(g, p, m):
        remote(held.at[g, p], g, p, m, 1, 0).wait_recv()

    def send(g, p):
        for index in range(len(DIRECT)):
            direct(g, p, index).start()

    for g in range(GROUPS):
        loads[g].wait()
        send(g, 0)
    for g in range(GROUPS):
        held[g, 1] = jnp.zeros((GV, W), F32)

    for load in small_loads:
        load.wait()

    lowest = R * me - REACH

    def find(n, carry):
        i = n // SPAN
        t = n - i * SPAN
        column = lax.rem(lowest + t + 192, 192)
        found = jnp.int32(-1)
        for k in range(K):
            found = jnp.where(pattern[i, k] == column, k, found)
        inverse[n] = found
        return carry

    lax.fori_loop(0, R * SPAN, find, 0)

    for load in tile_loads:
        load.wait()

    def build(j, carry):
        m = jnp.int32(0)
        for slot, source in enumerate(ORDER):
            m = jnp.where(j == slot, source, m)
        for b in range(R):
            rows = pl.ds(pl.multiple_of(j * W + b * B, B), B)
            for i in range(R):
                index = inverse[i * SPAN + R * m * sign + REACH + b]
                tile = tiles[i, jnp.maximum(index, 0)]
                tile = jnp.where(index >= 0, tile, 0.0)
                high, rest = split(tile.T)
                weights[rows, pl.ds(i * 2 * B, B)] = high
                weights[rows, pl.ds(i * 2 * B + B, B)] = rest
        return carry

    lax.fori_loop(0, len(ORDER), build, 0)

    def product(g, p):
        def chunk(first, count):
            pieces = []
            for j in range(first, first + count):
                pieces.append(held[g, p] if j == 0 else halo[g, p, j])
            return jnp.dot(
                stacked(pieces),
                weights[pl.ds(first * W, count * W), :],
                preferred_element_type=F32,
            )

        arrived(g, p, 1)
        total = chunk(0, 4)
        arrived(g, p, -1)
        arrived(g, p, 3)
        arrived(g, p, -4)
        total += chunk(4, 3)
        arrived(g, p, 4)
        arrived(g, p, -3)
        total += chunk(7, 2)
        columns = []
        for i in range(R):
            both = total[:, i * 2 * B : i * 2 * B + B] + total[:, i * 2 * B + B : (i + 1) * 2 * B]
            columns.append(both[:GV] + both[GV:])
        return jnp.concatenate(columns, axis=1)

    def pass_on(g, p):
        for index, (source, _) in enumerate(FORWARD):
            arrived(g, p, source)
            forward(g, p, index).start()

    def sent(g, p):
        for index in range(len(DIRECT)):
            direct(g, p, index).wait_send()
        for index in range(len(FORWARD)):
            forward(g, p, index).wait_send()

    center = center_ref[0]
    inverse_half = 1.0 / jnp.full((GV, W), half_ref[0], F32)

    def steps(n, carry):
        for p in (0, 1):
            factor = jnp.where(n * 2 + p == 0, 1.0, 2.0).astype(F32)
            for g in range(GROUPS):
                pass_on(g, p)
                applied = product(g, p)
                following = (
                    factor * (applied - center * held[g, p]) * inverse_half - held[g, 1 - p]
                )
                sent(g, p)
                held[g, 1 - p] = following
                send(g, 1 - p)
        return carry

    lax.fori_loop(0, DEG // 2, steps, 0)

    def to_next(g):
        return pltpu.make_async_remote_copy(
            src_ref=held.at[g, 0],
            dst_ref=low.at[g],
            send_sem=low_send.at[g],
            recv_sem=low_recv.at[g],
            device_id=cut_at(1),
            device_id_type=MESH,
        )

    for g in range(GROUPS):
        to_next(g).start()
    current = jnp.concatenate([held[g, 0] for g in range(GROUPS)], axis=0)

    def narrow(left, right):
        none = jnp.zeros((3 * V, W), F32)
        value = nt(left, jnp.concatenate([right, none], axis=0))
        return packed(value)

    def packed(value):
        total = value[:8]
        for q in range(1, 4):
            total = total + pltpu.roll(value[8 * q : 8 * q + 8], V * q, 1)
        return total

    def unpacked(value):
        parts = [value] + [pltpu.roll(value, 4 * V - V * q, 1) for q in range(1, 4)]
        return jnp.concatenate(parts, axis=0)

    def copies(a, phase):
        buffer, send_sems, recv_sems, own, device = phase
        count = buffer.shape[1]
        result = []
        for step in range(1, count):
            there = lax.rem(own + step, count)
            result.append(
                pltpu.make_async_remote_copy(
                    src_ref=buffer.at[a, own],
                    dst_ref=buffer.at[a, own],
                    send_sem=send_sems.at[a, step],
                    recv_sem=recv_sems.at[a, step],
                    device_id={"row": device(there)},
                    device_id_type=MESH,
                )
            )
        return result

    def begin(a, phase, value):
        phase[0][a, phase[3]] = value
        for copy in copies(a, phase):
            copy.start()

    def finish(a, phase):
        for copy in copies(a, phase):
            copy.wait()
        total = phase[0][a, 0]
        for n in range(1, phase[0].shape[1]):
            total = total + phase[0][a, n]
        return total

    along_z = (zbuf, z_send, z_recv, zpos, lambda z: (xpos * 8 + z) * 2 + core)
    along_x = (xbuf, x_send, x_recv, xpos, lambda x: (x * 8 + zpos) * 2 + core)
    in_chip = (cbuf, c_send, c_recv, core, lambda k: chip * 2 + k)

    GRAM, CROSS, QUOTIENT = 0, 1, 2
    begin(GRAM, along_z, narrow(current, current))
    pass_on(0, 0)
    imaged = [product(0, 0)]
    pass_on(1, 0)
    for g in range(GROUPS):
        to_next(g).wait()
    lower = jnp.concatenate([low[g] for g in range(GROUPS)], axis=0)
    begin(CROSS, along_z, narrow(current, lower))
    begin(GRAM, along_x, finish(GRAM, along_z))
    imaged.append(product(1, 0))
    begin(QUOTIENT, along_z, narrow(current, jnp.concatenate(imaged, axis=0)))
    for g in range(GROUPS):
        sent(g, 0)
    begin(CROSS, along_x, finish(CROSS, along_z))
    begin(GRAM, in_chip, finish(GRAM, along_x))
    gram = unpacked(finish(GRAM, in_chip))

    lane = lax.broadcasted_iota(jnp.int32, (V, 4 * V), 1)
    row = lax.broadcasted_iota(jnp.int32, (V, 4 * V), 0)
    table = jnp.where(lane < V, gram, jnp.where(lane == row + V, 1.0, 0.0))

    def eliminate(table, first, last):
        for j in range(first, last):
            scaled = table[j : j + 1, :] / table[j : j + 1, j : j + 1]
            table = table - jnp.where(row > j, table[:, j : j + 1] * scaled, 0.0)
        return table

    table = eliminate(table, 0, V // 2)
    begin(QUOTIENT, along_x, finish(QUOTIENT, along_z))
    table = eliminate(table, V // 2, V - 1)
    diagonal = jnp.sum(jnp.where(lane == row, table, 0.0), axis=1, keepdims=True)
    table = jnp.where(lane < V, 0.0, table) / jnp.sqrt(diagonal)
    table = pltpu.roll(table, 3 * V, 1)
    factor_buf[0] = packed(table)
    factor_copy = pltpu.make_async_remote_copy(
        src_ref=factor_buf.at[0],
        dst_ref=factor_buf.at[1],
        send_sem=factor_sem.at[0],
        recv_sem=factor_sem.at[1],
        device_id=cut_at(1),
        device_id_type=MESH,
    )
    factor_copy.start()
    factor_inverse = table[:, :V]
    begin(CROSS, in_chip, finish(CROSS, along_x))
    basis = nn(factor_inverse, current)
    small_row = lax.broadcasted_iota(jnp.int32, (V, V), 0)
    small_lane = lax.broadcasted_iota(jnp.int32, (V, V), 1)
    chosen = jnp.zeros((V, V), F32)
    for p in range(8):
        chosen += jnp.where(
            (small_row == pairs[0, 0, p]) & (small_lane == pairs[0, 1, p]), 1.0, 0.0
        )
    begin(QUOTIENT, in_chip, finish(QUOTIENT, along_x))
    cross = nn(factor_inverse, unpacked(finish(CROSS, in_chip))[:, :V])
    factor_copy.wait()
    lower_inverse = unpacked(factor_buf[1])[:, :V]
    lower_basis = jnp.where(cut > 0, nn(lower_inverse, lower), 0.0)
    removed = jnp.where(cut > 0, chosen * nt(cross, lower_inverse), 0.0)
    out_ref[0] = math.sqrt(order_total) * (basis - nn(removed, lower_basis))
    quotient = unpacked(finish(QUOTIENT, in_chip))[:, :V]
    proj_ref[0] = nt(nn(factor_inverse, quotient), factor_inverse)


def write(filtered, quotient, out_ref, proj_ref, sem):
    copies = [
        pltpu.make_async_copy(filtered, out_ref, sem.at[0]),
        pltpu.make_async_copy(quotient, proj_ref, sem.at[1]),
    ]
    for copy in copies:
        copy.start()
    for copy in copies:
        copy.wait()


def local(block_tiles, tile_pattern, start_vectors, centers, halfwidths, dup_pairs):
    order_total = start_vectors.shape[2] * lax.axis_size("row")
    vmem = pl.BlockSpec(memory_space=pltpu.VMEM)
    hbm = pl.BlockSpec(memory_space=pltpu.HBM)
    dma = pltpu.SemaphoreType.DMA
    fixed = lambda operand: pltpu.with_memory_space_constraint(operand, pltpu.HBM)
    shapes = (
        jax.ShapeDtypeStruct((1, V, W), F32),
        jax.ShapeDtypeStruct((1, V, V), F32),
    )
    results = pl.pallas_call(
        functools.partial(kernel, order_total),
        out_shape=shapes,
        in_specs=[hbm] * 6,
        out_specs=(vmem, vmem),
        scratch_shapes=[
            pltpu.SMEM((R, K), jnp.int32),
            pltpu.SMEM((1,), F32),
            pltpu.SMEM((1,), F32),
            pltpu.SMEM((1, 2, 8), jnp.int32),
            pltpu.VMEM((R, K, B, B), F32),
            pltpu.VMEM((9 * W, 2 * W), BF16),
            pltpu.SMEM((R * SPAN,), jnp.int32),
            pltpu.VMEM((GROUPS, 2, GV, W), F32),
            pltpu.VMEM((GROUPS, 2, 9, GV, W), F32),
            pltpu.VMEM((GROUPS, GV, W), F32),
            pltpu.VMEM((3, 8, 8, 4 * V), F32),
            pltpu.VMEM((3, 4, 8, 4 * V), F32),
            pltpu.VMEM((3, 2, 8, 4 * V), F32),
            dma((R,)),
            dma((GROUPS,)),
            dma((GROUPS, NSEND)),
            dma((GROUPS, 2, 9)),
            dma((GROUPS,)),
            dma((GROUPS,)),
            dma((3, 8)),
            dma((3, 8)),
            dma((3, 4)),
            dma((3, 4)),
            dma((3, 2)),
            dma((3, 2)),
            pltpu.VMEM((2, 8, 4 * V), F32),
            dma((2,)),
            dma((4,)),
        ],
        compiler_params=pltpu.CompilerParams(
            collective_id=0, has_side_effects=True, vmem_limit_bytes=52 << 20
        ),
    )(
        fixed(block_tiles),
        fixed(tile_pattern),
        fixed(start_vectors),
        centers,
        halfwidths,
        fixed(jnp.transpose(dup_pairs, (0, 2, 1))),
    )
    return pl.pallas_call(
        write,
        out_shape=shapes,
        in_specs=[pl.BlockSpec(memory_space=pl.ANY)] * 2,
        out_specs=(hbm, hbm),
        scratch_shapes=[dma((2,))],
        compiler_params=pltpu.CompilerParams(vmem_limit_bytes=1 << 20),
    )(*results)


def solution(mesh):
    in_specs = (
        P("row", None, None, None),
        P("row", None),
        P("cuts", None, "row"),
        P("cuts"),
        P("cuts"),
        P("cuts", None, None),
    )
    out_specs = (P("cuts", None, "row"), P("cuts", None, None))
    return jax.shard_map(local, mesh=mesh, in_specs=in_specs, out_specs=out_specs, check_vma=False)
```

```python
import functools
import math

import jax
import jax.numpy as jnp
from jax import lax
from jax.experimental import pallas as pl
from jax.experimental.pallas import tpu as pltpu
from jax.sharding import PartitionSpec as P

DEG = 8
REACH = 12
B = 128
K = 24
R = 3
SPAN = R * 9
V = 32
GROUPS = 2
GV = V // GROUPS
W = R * B
MESH = pl.DeviceIdType.MESH
HIGH = lax.Precision.HIGHEST
F32 = jnp.float32
BF16 = jnp.bfloat16

ORDER = (0, 1, 2, -2, -1, 3, -4, 4, -3)
SLOT = {m: i for i, m in enumerate(ORDER)}
DIRECT = ((2, -2), (-2, 2), (-1, -1), (3, 3), (4, -4), (-4, 4), (-3, -3), (1, 1))
FORWARD = ()
NSEND = len(DIRECT) + len(FORWARD)


def split(values):
    high = values.astype(BF16)
    low = (values - high.astype(F32)).astype(BF16)
    return high, low


def stacked(pieces):
    columns = []
    for piece in pieces:
        columns.append(jnp.concatenate(split(piece), axis=0))
    return jnp.concatenate(columns, axis=1)


def nt(a, b):
    return lax.dot_general(
        a, b, (((1,), (1,)), ((), ())), precision=HIGH, preferred_element_type=F32
    )


def nn(a, b):
    return jnp.dot(a, b, precision=HIGH, preferred_element_type=F32)


def kernel(
    order_total,
    tiles_hbm,
    pattern_hbm,
    start_hbm,
    center_hbm,
    half_hbm,
    pairs_hbm,
    out_ref,
    proj_ref,
    pattern,
    center_ref,
    half_ref,
    pairs,
    tiles,
    weights,
    inverse,
    held,
    halo,
    low,
    zbuf,
    xbuf,
    cbuf,
    tile_sem,
    start_sem,
    send_sem,
    recv_sem,
    low_send,
    low_recv,
    z_send,
    z_recv,
    x_send,
    x_recv,
    c_send,
    c_recv,
    factor_buf,
    factor_sem,
    small_sem,
):
    me = lax.axis_index("row")
    cut = lax.axis_index("cuts")
    core = lax.rem(me, 2)
    chip = me // 2
    zpos = lax.rem(chip, 8)
    xpos = chip // 8
    sign = 1 - 2 * core

    def at(m):
        return {"row": lax.rem(me + m * sign + 64, 64)}

    def cut_at(step):
        return {"cuts": lax.rem(cut + step + 8, 8)}

    small_loads = []
    for n, (source, target) in enumerate(
        (
            (pattern_hbm, pattern),
            (center_hbm, center_ref),
            (half_hbm, half_ref),
            (pairs_hbm, pairs),
        )
    ):
        load = pltpu.make_async_copy(source, target, small_sem.at[n])
        load.start()
        small_loads.append(load)
    loads = []
    for g in range(GROUPS):
        load = pltpu.make_async_copy(
            start_hbm.at[0, pl.ds(g * GV, GV), :], held.at[g, 0], start_sem.at[g]
        )
        load.start()
        loads.append(load)
    tile_loads = []
    for i in range(R):
        load = pltpu.make_async_copy(tiles_hbm.at[i], tiles.at[i], tile_sem.at[i])
        load.start()
        tile_loads.append(load)

    barrier = pltpu.get_barrier_semaphore()
    for m in (-4, -3, -2, -1, 1, 2, 3, 4):
        pl.semaphore_signal(barrier, inc=1, device_id=at(m), device_id_type=MESH)
    for step in (-1, 1):
        pl.semaphore_signal(barrier, inc=1, device_id=cut_at(step), device_id_type=MESH)
    pl.semaphore_wait(barrier, 10)

    def remote(src, g, p, coordinate, target, index):
        return pltpu.make_async_remote_copy(
            src_ref=src,
            dst_ref=halo.at[g, p, SLOT[coordinate]],
            send_sem=send_sem.at[g, index],
            recv_sem=recv_sem.at[g, p, SLOT[coordinate]],
            device_id=at(target),
            device_id_type=MESH,
        )

    def direct(g, p, index):
        target, coordinate = DIRECT[index]
        return remote(held.at[g, p], g, p, coordinate, target, index)

    def forward(g, p, index):
        source, coordinate = FORWARD[index]
        return remote(
            halo.at[g, p, SLOT[source]], g, p, coordinate, 1, len(DIRECT) + index
        )

    def arrived(g, p, m):
        remote(held.at[g, p], g, p, m, 1, 0).wait_recv()

    def send(g, p):
        for index in range(len(DIRECT)):
            direct(g, p, index).start()

    for g in range(GROUPS):
        loads[g].wait()
        send(g, 0)
    for g in range(GROUPS):
        held[g, 1] = jnp.zeros((GV, W), F32)

    for load in small_loads:
        load.wait()

    lowest = R * me - REACH

    def find(n, carry):
        i = n // SPAN
        t = n - i * SPAN
        column = lax.rem(lowest + t + 192, 192)
        found = jnp.int32(-1)
        for k in range(K):
            found = jnp.where(pattern[i, k] == column, k, found)
        inverse[n] = found
        return carry

    lax.fori_loop(0, R * SPAN, find, 0)

    for load in tile_loads:
        load.wait()

    def build(j, carry):
        m = jnp.int32(0)
        for slot, source in enumerate(ORDER):
            m = jnp.where(j == slot, source, m)
        for b in range(R):
            rows = pl.ds(pl.multiple_of(j * W + b * B, B), B)
            for i in range(R):
                index = inverse[i * SPAN + R * m * sign + REACH + b]
                tile = tiles[i, jnp.maximum(index, 0)]
                tile = jnp.where(index >= 0, tile, 0.0)
                high, rest = split(tile.T)
                weights[rows, pl.ds(i * 2 * B, B)] = high
                weights[rows, pl.ds(i * 2 * B + B, B)] = rest
        return carry

    lax.fori_loop(0, len(ORDER), build, 0)

    def product(g, p):
        def chunk(first, count):
            pieces = []
            for j in range(first, first + count):
                pieces.append(held[g, p] if j == 0 else halo[g, p, j])
            return jnp.dot(
                stacked(pieces),
                weights[pl.ds(first * W, count * W), :],
                preferred_element_type=F32,
            )

        arrived(g, p, 1)
        arrived(g, p, 2)
        arrived(g, p, -2)
        total = chunk(0, 4)
        arrived(g, p, -1)
        arrived(g, p, 3)
        arrived(g, p, -4)
        total += chunk(4, 3)
        arrived(g, p, 4)
        arrived(g, p, -3)
        total += chunk(7, 2)
        columns = []
        for i in range(R):
            both = total[:, i * 2 * B : i * 2 * B + B] + total[:, i * 2 * B + B : (i + 1) * 2 * B]
            columns.append(both[:GV] + both[GV:])
        return jnp.concatenate(columns, axis=1)

    def pass_on(g, p):
        for index, (source, _) in enumerate(FORWARD):
            arrived(g, p, source)
            forward(g, p, index).start()

    def sent(g, p):
        for index in range(len(DIRECT)):
            direct(g, p, index).wait_send()
        for index in range(len(FORWARD)):
            forward(g, p, index).wait_send()

    center = center_ref[0]
    inverse_half = 1.0 / jnp.full((GV, W), half_ref[0], F32)

    def steps(n, carry):
        for p in (0, 1):
            factor = jnp.where(n * 2 + p == 0, 1.0, 2.0).astype(F32)
            for g in range(GROUPS):
                pass_on(g, p)
                applied = product(g, p)
                following = (
                    factor * (applied - center * held[g, p]) * inverse_half - held[g, 1 - p]
                )
                sent(g, p)
                held[g, 1 - p] = following
                send(g, 1 - p)
        return carry

    lax.fori_loop(0, DEG // 2, steps, 0)

    def to_next(g):
        return pltpu.make_async_remote_copy(
            src_ref=held.at[g, 0],
            dst_ref=low.at[g],
            send_sem=low_send.at[g],
            recv_sem=low_recv.at[g],
            device_id=cut_at(1),
            device_id_type=MESH,
        )

    for g in range(GROUPS):
        to_next(g).start()
    current = jnp.concatenate([held[g, 0] for g in range(GROUPS)], axis=0)

    def narrow(left, right):
        none = jnp.zeros((3 * V, W), F32)
        value = nt(left, jnp.concatenate([right, none], axis=0))
        return packed(value)

    def packed(value):
        total = value[:8]
        for q in range(1, 4):
            total = total + pltpu.roll(value[8 * q : 8 * q + 8], V * q, 1)
        return total

    def unpacked(value):
        parts = [value] + [pltpu.roll(value, 4 * V - V * q, 1) for q in range(1, 4)]
        return jnp.concatenate(parts, axis=0)

    def copies(a, phase):
        buffer, send_sems, recv_sems, own, device = phase
        count = buffer.shape[1]
        result = []
        for step in range(1, count):
            there = lax.rem(own + step, count)
            result.append(
                pltpu.make_async_remote_copy(
                    src_ref=buffer.at[a, own],
                    dst_ref=buffer.at[a, own],
                    send_sem=send_sems.at[a, step],
                    recv_sem=recv_sems.at[a, step],
                    device_id={"row": device(there)},
                    device_id_type=MESH,
                )
            )
        return result

    def begin(a, phase, value):
        phase[0][a, phase[3]] = value
        for copy in copies(a, phase):
            copy.start()

    def finish(a, phase):
        for copy in copies(a, phase):
            copy.wait()
        total = phase[0][a, 0]
        for n in range(1, phase[0].shape[1]):
            total = total + phase[0][a, n]
        return total

    along_z = (zbuf, z_send, z_recv, zpos, lambda z: (xpos * 8 + z) * 2 + core)
    along_x = (xbuf, x_send, x_recv, xpos, lambda x: (x * 8 + zpos) * 2 + core)
    in_chip = (cbuf, c_send, c_recv, core, lambda k: chip * 2 + k)

    GRAM, CROSS, QUOTIENT = 0, 1, 2
    begin(GRAM, along_z, narrow(current, current))
    pass_on(0, 0)
    imaged = [product(0, 0)]
    pass_on(1, 0)
    for g in range(GROUPS):
        to_next(g).wait()
    lower = jnp.concatenate([low[g] for g in range(GROUPS)], axis=0)
    begin(CROSS, along_z, narrow(current, lower))
    begin(GRAM, along_x, finish(GRAM, along_z))
    imaged.append(product(1, 0))
    begin(QUOTIENT, along_z, narrow(current, jnp.concatenate(imaged, axis=0)))
    for g in range(GROUPS):
        sent(g, 0)
    begin(CROSS, along_x, finish(CROSS, along_z))
    begin(GRAM, in_chip, finish(GRAM, along_x))
    gram = unpacked(finish(GRAM, in_chip))

    lane = lax.broadcasted_iota(jnp.int32, (V, 4 * V), 1)
    row = lax.broadcasted_iota(jnp.int32, (V, 4 * V), 0)
    table = jnp.where(lane < V, gram, jnp.where(lane == row + V, 1.0, 0.0))

    def eliminate(table, first, last):
        for j in range(first, last):
            scaled = table[j : j + 1, :] / table[j : j + 1, j : j + 1]
            table = table - jnp.where(row > j, table[:, j : j + 1] * scaled, 0.0)
        return table

    table = eliminate(table, 0, V // 2)
    begin(QUOTIENT, along_x, finish(QUOTIENT, along_z))
    table = eliminate(table, V // 2, V - 1)
    diagonal = jnp.sum(jnp.where(lane == row, table, 0.0), axis=1, keepdims=True)
    table = jnp.where(lane < V, 0.0, table) / jnp.sqrt(diagonal)
    table = pltpu.roll(table, 3 * V, 1)
    factor_buf[0] = packed(table)
    factor_copy = pltpu.make_async_remote_copy(
        src_ref=factor_buf.at[0],
        dst_ref=factor_buf.at[1],
        send_sem=factor_sem.at[0],
        recv_sem=factor_sem.at[1],
        device_id=cut_at(1),
        device_id_type=MESH,
    )
    factor_copy.start()
    factor_inverse = table[:, :V]
    begin(CROSS, in_chip, finish(CROSS, along_x))
    basis = nn(factor_inverse, current)
    small_row = lax.broadcasted_iota(jnp.int32, (V, V), 0)
    small_lane = lax.broadcasted_iota(jnp.int32, (V, V), 1)
    chosen = jnp.zeros((V, V), F32)
    for p in range(8):
        chosen += jnp.where(
            (small_row == pairs[0, 0, p]) & (small_lane == pairs[0, 1, p]), 1.0, 0.0
        )
    begin(QUOTIENT, in_chip, finish(QUOTIENT, along_x))
    cross = nn(factor_inverse, unpacked(finish(CROSS, in_chip))[:, :V])
    factor_copy.wait()
    lower_inverse = unpacked(factor_buf[1])[:, :V]
    lower_basis = jnp.where(cut > 0, nn(lower_inverse, lower), 0.0)
    removed = jnp.where(cut > 0, chosen * nt(cross, lower_inverse), 0.0)
    out_ref[0] = math.sqrt(order_total) * (basis - nn(removed, lower_basis))
    quotient = unpacked(finish(QUOTIENT, in_chip))[:, :V]
    proj_ref[0] = nt(nn(factor_inverse, quotient), factor_inverse)


def write(filtered, quotient, out_ref, proj_ref, sem):
    copies = [
        pltpu.make_async_copy(filtered, out_ref, sem.at[0]),
        pltpu.make_async_copy(quotient, proj_ref, sem.at[1]),
    ]
    for copy in copies:
        copy.start()
    for copy in copies:
        copy.wait()


def local(block_tiles, tile_pattern, start_vectors, centers, halfwidths, dup_pairs):
    order_total = start_vectors.shape[2] * lax.axis_size("row")
    vmem = pl.BlockSpec(memory_space=pltpu.VMEM)
    hbm = pl.BlockSpec(memory_space=pltpu.HBM)
    dma = pltpu.SemaphoreType.DMA
    fixed = lambda operand: pltpu.with_memory_space_constraint(operand, pltpu.HBM)
    shapes = (
        jax.ShapeDtypeStruct((1, V, W), F32),
        jax.ShapeDtypeStruct((1, V, V), F32),
    )
    results = pl.pallas_call(
        functools.partial(kernel, order_total),
        out_shape=shapes,
        in_specs=[hbm] * 6,
        out_specs=(vmem, vmem),
        scratch_shapes=[
            pltpu.SMEM((R, K), jnp.int32),
            pltpu.SMEM((1,), F32),
            pltpu.SMEM((1,), F32),
            pltpu.SMEM((1, 2, 8), jnp.int32),
            pltpu.VMEM((R, K, B, B), F32),
            pltpu.VMEM((9 * W, 2 * W), BF16),
            pltpu.SMEM((R * SPAN,), jnp.int32),
            pltpu.VMEM((GROUPS, 2, GV, W), F32),
            pltpu.VMEM((GROUPS, 2, 9, GV, W), F32),
            pltpu.VMEM((GROUPS, GV, W), F32),
            pltpu.VMEM((3, 8, 8, 4 * V), F32),
            pltpu.VMEM((3, 4, 8, 4 * V), F32),
            pltpu.VMEM((3, 2, 8, 4 * V), F32),
            dma((R,)),
            dma((GROUPS,)),
            dma((GROUPS, NSEND)),
            dma((GROUPS, 2, 9)),
            dma((GROUPS,)),
            dma((GROUPS,)),
            dma((3, 8)),
            dma((3, 8)),
            dma((3, 4)),
            dma((3, 4)),
            dma((3, 2)),
            dma((3, 2)),
            pltpu.VMEM((2, 8, 4 * V), F32),
            dma((2,)),
            dma((4,)),
        ],
        compiler_params=pltpu.CompilerParams(
            collective_id=0, has_side_effects=True, vmem_limit_bytes=52 << 20
        ),
    )(
        fixed(block_tiles),
        fixed(tile_pattern),
        fixed(start_vectors),
        centers,
        halfwidths,
        fixed(jnp.transpose(dup_pairs, (0, 2, 1))),
    )
    return pl.pallas_call(
        write,
        out_shape=shapes,
        in_specs=[pl.BlockSpec(memory_space=pl.ANY)] * 2,
        out_specs=(hbm, hbm),
        scratch_shapes=[dma((2,))],
        compiler_params=pltpu.CompilerParams(vmem_limit_bytes=1 << 20),
    )(*results)


def solution(mesh):
    in_specs = (
        P("row", None, None, None),
        P("row", None),
        P("cuts", None, "row"),
        P("cuts"),
        P("cuts"),
        P("cuts", None, None),
    )
    out_specs = (P("cuts", None, "row"), P("cuts", None, None))
    return jax.shard_map(local, mesh=mesh, in_specs=in_specs, out_specs=out_specs, check_vma=False)
```
